256 devices in a mesh: seq: 16 (over x, y), dp: 16 (over z, core).
Axes of the slice: x: 4, y: 4, z: 8, core: 2. Of those that a mesh axis runs over, the one named last changes fastest.
Arguments:
- query_rows: bfloat16 [16, 4096, 2048], P('dp', 'seq'), may hold values from -22 to 22
- key_rows: bfloat16 [16, 4096, 2048], P('dp', 'seq'), may hold values from -7 to 7
- value_rows: bfloat16 [16, 4096, 2048], P('dp', 'seq'), may hold values from -6 to 6
- sink_logit: float32 [16], replicated, may hold values from 6 to 11
- grad_out: bfloat16 [16, 4096, 2048], P('dp', 'seq'), may hold values from -1.6 to 1.6
- pattern: int32 [16, 32, 8], replicated, may hold values from 0 to 31, as said below
Outputs:
- attended: bfloat16 [16, 4096, 2048], P('dp', 'seq')
- grad_query: bfloat16 [16, 4096, 2048], P('dp', 'seq')
- grad_key: bfloat16 [16, 4096, 2048], P('dp', 'seq')
- grad_value: bfloat16 [16, 4096, 2048], P('dp', 'seq')
- grad_sink: float32 [16], replicated
The draws below stay inside these ranges and needn't reach their ends.
Inputs may be any that keep to these rules, and one draw needn't show every extreme that they name: For each head h and query block b, pattern[h, b] lists 8 distinct key blocks: the three neighbouring blocks b - 1, b, b + 1 (moved inward at the ends of the document), the first and the last block, and blocks drawn at random to fill the row.
All inputs are finite; a program needn't handle non-finite values.
Results may differ from the reference program's by a relative error of at most 0.012.
The reference program's roundings to bfloat16 on the way count: a program that leaves them out, or rounds other values in their place, can miss the bound.
Values may be sent and summed in bfloat16 or wider, within the bound.
No kernel may reach another device: no remote copies, remote signals or barrier semaphores. Data moves between devices by JAX's collectives and lax.ppermute only.
A program may use at most 64 MiB of HBM per device.

```python
import jax
import jax.numpy as jnp
from jax import lax

H = 16
HEAD = 128
BLOCK = 128
KB = 8
DOCS = 16
SEQLEN = 4096
NB = 32


def base_keys(key):
    shape = (DOCS, SEQLEN, H * HEAD)
    return jnp.clip(jax.random.normal(jax.random.fold_in(key, 7), shape, jnp.float32), -4.0, 4.0)


def draw_key_rows(key, part):
    return base_keys(key).astype(jnp.bfloat16)


def draw_query_rows(key, part):
    shape = (DOCS, SEQLEN, H * HEAD)
    raw = jnp.clip(jax.random.normal(jax.random.fold_in(key, 21), shape, jnp.float32), -4.0, 4.0)
    return (2.5 * raw).astype(jnp.bfloat16)


def draw_grad_out(key, part):
    shape = (DOCS, SEQLEN, H * HEAD)
    rising = jnp.arange(DOCS, dtype=jnp.float32)[:, None, None] / max(DOCS - 1, 1)
    raw = jnp.clip(jax.random.normal(jax.random.fold_in(key, 31), shape, jnp.float32), -4.0, 4.0)
    return (0.1 * (1.0 + 2.0 * rising) * raw).astype(jnp.bfloat16)


def draw_pattern(key, part):
    blocks = jnp.arange(NB)
    start = jnp.clip(blocks - 1, 0, NB - 3)
    window = (blocks[None, :] >= start[:, None]) & (blocks[None, :] < start[:, None] + 3)
    globe = (blocks == 0) | (blocks == NB - 1)
    special = (window | globe[None, :]).astype(jnp.int32)
    subkeys = jax.random.split(jax.random.fold_in(key, 41), H * NB)
    orders = jax.vmap(lambda single: jax.random.permutation(single, NB))(subkeys).reshape(H, NB, NB)
    ranking = special[None, :, :] * (2 * NB) + orders.astype(jnp.int32)
    _, chosen = lax.top_k(ranking, KB)
    return chosen.astype(jnp.int32)


def levels(rng, dims, shards, least, largest):
    factor_of = 1.0
    for position, shards_of in shards:
        heights = jax.random.uniform(jax.random.fold_in(jax.random.fold_in(rng, 6), position), (shards_of,), jnp.float32, least / len(shards), largest / len(shards))
        factor_of = factor_of * jnp.repeat(jnp.exp(heights), dims[position] // shards_of).reshape((-1,) + (1,) * (len(dims) - 1 - position))
    return factor_of


def centred(key, shape, spread, reach, shards=(), kind=jnp.bfloat16):
    array = spread * jax.random.normal(key, shape, jnp.float32)
    if shards:
        array = array * levels(key, shape, shards, -0.22, 0.18)
    return jnp.clip(array, -reach, reach).astype(kind)


def setup_inputs(seed: int = 0) -> dict:
    key_of = jax.random.split(jax.random.key(seed), 7)
    query_rows = draw_query_rows(jax.random.fold_in(key_of[6], 71), 0)
    key_rows = draw_key_rows(jax.random.fold_in(key_of[6], 71), 0)
    value_rows = centred(key_of[2], (DOCS, SEQLEN, H * HEAD), 1.0, 6.0, ((0, 16), (1, 16)))
    sink_logit = jnp.clip(jax.random.uniform(key_of[3], (H,), jnp.float32, 6.0, 11.0), 6.0, 11.0)
    grad_out = draw_grad_out(jax.random.fold_in(key_of[6], 71), 0)
    pattern = draw_pattern(jax.random.fold_in(key_of[6], 71), 0)
    return dict(query_rows=query_rows, key_rows=key_rows, value_rows=value_rows, sink_logit=sink_logit, grad_out=grad_out, pattern=pattern)


def head_pass(query_head, key_head, value_head, grad_head, link_rows, sink_value):
    block_count = query_head.shape[0] // BLOCK
    scaling = HEAD ** -0.5
    queries = query_head.reshape(block_count, BLOCK, HEAD).astype(jnp.float32)
    key_tiles = key_head.reshape(block_count, BLOCK, HEAD)[link_rows].astype(jnp.float32)
    value_tiles = value_head.reshape(block_count, BLOCK, HEAD)[link_rows].astype(jnp.float32)
    grads = grad_head.reshape(block_count, BLOCK, HEAD).astype(jnp.float32)
    scores = jnp.einsum("nqe,nkbe->nqkb", queries, key_tiles) * scaling
    row_top = jnp.maximum(jnp.max(scores, axis=(2, 3)), sink_value)
    summed = jnp.sum(jnp.exp(scores - row_top[:, :, None, None]), axis=(2, 3)) + jnp.exp(sink_value - row_top)
    log_total = row_top + jnp.log(summed)
    weights = jnp.exp(scores - log_total[:, :, None, None])
    rounded = lax.optimization_barrier(weights.astype(jnp.bfloat16)).astype(jnp.float32)
    attended = jnp.einsum("nqkb,nkbe->nqe", rounded, value_tiles).astype(jnp.bfloat16)
    attended_wide = lax.optimization_barrier(attended).astype(jnp.float32)
    row_dot = jnp.sum(grads * attended_wide, axis=-1)
    grad_weights = jnp.einsum("nqe,nkbe->nqkb", grads, value_tiles)
    grad_scores = (weights * (grad_weights - row_dot[:, :, None, None])).astype(jnp.bfloat16)
    grad_scores = lax.optimization_barrier(grad_scores).astype(jnp.float32)
    grad_query = (jnp.einsum("nqkb,nkbe->nqe", grad_scores, key_tiles) * scaling).astype(jnp.bfloat16)
    key_part = jnp.einsum("nqkb,nqe->nkbe", grad_scores, queries) * scaling
    value_part = jnp.einsum("nqkb,nqe->nkbe", rounded, grads)
    flat_links = link_rows.reshape(-1).astype(jnp.int32)
    grad_key = jnp.zeros((block_count, BLOCK, HEAD), jnp.float32).at[flat_links].add(key_part.reshape(-1, BLOCK, HEAD))
    grad_value = jnp.zeros((block_count, BLOCK, HEAD), jnp.float32).at[flat_links].add(value_part.reshape(-1, BLOCK, HEAD))
    sink_term = -jnp.sum(jnp.exp(sink_value - log_total) * row_dot)
    return (attended.reshape(-1, HEAD), grad_query.reshape(-1, HEAD),
            grad_key.astype(jnp.bfloat16).reshape(-1, HEAD), grad_value.astype(jnp.bfloat16).reshape(-1, HEAD), sink_term)


def by_head(array_in):
    return jnp.transpose(array_in.reshape(SEQLEN, H, HEAD), (1, 0, 2))


def by_token(array_in):
    return jnp.transpose(array_in, (1, 0, 2)).reshape(SEQLEN, H * HEAD)


def reference(query_rows, key_rows, value_rows, sink_logit, grad_out, pattern):
    def per_document(inputs):
        query_doc, key_doc, value_doc, grad_doc = inputs
        results = lax.map(lambda packed: head_pass(*packed),
                          (by_head(query_doc), by_head(key_doc), by_head(value_doc), by_head(grad_doc), pattern, sink_logit))
        return by_token(results[0]), by_token(results[1]), by_token(results[2]), by_token(results[3]), results[4]

    outputs = lax.map(per_document, (query_rows, key_rows, value_rows, grad_out))
    grad_sink = jnp.sum(outputs[4], axis=0) / DOCS
    return outputs[0], outputs[1], outputs[2], outputs[3], grad_sink
```

```python
import functools

import jax
import jax.numpy as jnp
from jax import lax
from jax.experimental import pallas as pl
from jax.experimental.pallas import tpu as pltpu
from jax.sharding import PartitionSpec as P

HEAD = 128
BLOCK = 128
LOG2E = 1.4426950408889634
F32 = jnp.float32
BF16 = jnp.bfloat16

NT = (((1,), (1,)), ((), ()))
NN = (((1,), (0,)), ((), ()))
VMEM_WHOLE = pl.BlockSpec(memory_space=pltpu.VMEM)
SMEM_WHOLE = pl.BlockSpec(memory_space=pltpu.SMEM)
IN_PLACE = pl.BlockSpec(memory_space=pl.ANY)


def dot(left, right, dims):
    return lax.dot_general(left, right, dims, preferred_element_type=F32)


def tile(ref, block, part, per_device):
    rows = per_device * BLOCK
    half = lax.rem(block, per_device)
    start = pl.multiple_of(part * rows + half * BLOCK, BLOCK)
    return ref.at[lax.div(block, per_device), pl.ds(start, BLOCK), :]


def forward_kernel(blocks, slots, per_device, scaling, links, sink, rows, out, weights, sink_weight,
                   value_t, score):
    sink_value = sink[0]

    def flip(c, carry):
        value_t[c] = tile(rows, c, 2, per_device)[...].T
        return carry

    lax.fori_loop(0, blocks, flip, 0)

    def one_block(b, carry):
        queries = tile(rows, b, 0, per_device)[...]
        chosen = [links[b * slots + j] for j in range(slots)]
        top = None
        for j, c in enumerate(chosen):
            part = dot(tile(rows, c, 1, per_device)[...], queries, NT)
            score[pl.ds(j * BLOCK, BLOCK), :] = part
            part_top = jnp.max(part, axis=0, keepdims=True)
            top = part_top if top is None else jnp.maximum(top, part_top)
        top = jnp.maximum(top * scaling, sink_value)
        shift = top * LOG2E
        total = jnp.exp(sink_value - top)
        sink_part = total
        for j in range(slots):
            part = jnp.exp2(score[pl.ds(j * BLOCK, BLOCK), :] * (scaling * LOG2E) - shift)
            score[pl.ds(j * BLOCK, BLOCK), :] = part
            total = total + jnp.sum(part, axis=0, keepdims=True)
        inverse = 1.0 / total
        for j in range(slots):
            weights[b, pl.ds(j * BLOCK, BLOCK), :] = (
                score[pl.ds(j * BLOCK, BLOCK), :] * inverse).astype(BF16)
        values = jnp.concatenate([value_t[c] for c in chosen], axis=1)
        result = dot(values, weights[b], NN)
        tile(out, b, 0, per_device)[...] = result.T.astype(BF16)
        sink_weight[pl.ds(b, 1), :] = sink_part * inverse
        return carry

    lax.fori_loop(0, blocks, one_block, 0)


def backward_kernel(blocks, slots, per_device, scaling, links, rows, grads, attended, weights,
                    sink_weight, out, sink_out, key_t, change, key_sum, value_sum):
    def prepare(c, carry):
        key_t[c] = tile(rows, c, 1, per_device)[...].T
        key_sum[c] = jnp.zeros((BLOCK, HEAD), F32)
        value_sum[c] = jnp.zeros((BLOCK, HEAD), F32)
        return carry

    lax.fori_loop(0, blocks, prepare, 0)

    def one_block(b, sink_total):
        queries = tile(rows, b, 0, per_device)[...]
        grad = tile(grads, b, 0, per_device)[...]
        result = tile(attended, b, 0, per_device)[...]
        product = grad.astype(F32) * result.astype(F32)
        row_dot = jnp.sum(product.T, axis=0, keepdims=True)
        chosen = [links[b * slots + j] for j in range(slots)]
        for j, c in enumerate(chosen):
            weight = weights[b, pl.ds(j * BLOCK, BLOCK), :]
            grad_weight = dot(tile(rows, c, 2, per_device)[...], grad, NT)
            delta = (weight.astype(F32) * (grad_weight - row_dot)).astype(BF16)
            change[pl.ds(j * BLOCK, BLOCK), :] = delta
            value_sum[c] += dot(weight, grad, NN)
            key_sum[c] += dot(delta, queries, NN)
        keys = jnp.concatenate([key_t[c] for c in chosen], axis=1)
        grad_query = dot(keys, change[...], NN) * scaling
        tile(out, b, 0, per_device)[...] = grad_query.T.astype(BF16)
        return sink_total + row_dot * sink_weight[pl.ds(b, 1), :]

    sink_total = lax.fori_loop(0, blocks, one_block, jnp.zeros((1, BLOCK), F32))
    sink_out[...] = jnp.broadcast_to(sink_total, sink_out.shape)

    def finish(c, carry):
        tile(out, c, 1, per_device)[...] = (key_sum[c] * scaling).astype(BF16)
        tile(out, c, 2, per_device)[...] = value_sum[c].astype(BF16)
        return carry

    lax.fori_loop(0, blocks, finish, 0)


def forward(links, sink, rows, scaling, slots):
    peers, depth, _ = rows.shape
    tokens = depth // 3
    per_device = tokens // BLOCK
    blocks = peers * per_device
    return pl.pallas_call(
        functools.partial(forward_kernel, blocks, slots, per_device, scaling),
        out_shape=(
            jax.ShapeDtypeStruct((peers, tokens, HEAD), BF16),
            jax.ShapeDtypeStruct((blocks, slots * BLOCK, BLOCK), BF16),
            jax.ShapeDtypeStruct((blocks, BLOCK), F32),
        ),
        in_specs=[SMEM_WHOLE, SMEM_WHOLE, VMEM_WHOLE],
        out_specs=(VMEM_WHOLE, VMEM_WHOLE, VMEM_WHOLE),
        scratch_shapes=[
            pltpu.VMEM((blocks, HEAD, BLOCK), BF16),
            pltpu.VMEM((slots * BLOCK, BLOCK), F32),
        ],
        compiler_params=pltpu.CompilerParams(vmem_limit_bytes=40 << 20),
        cost_estimate=pl.CostEstimate(
            flops=4 * blocks * slots * BLOCK * BLOCK * HEAD,
            bytes_accessed=14 << 20,
            transcendentals=blocks * slots * BLOCK * BLOCK,
        ),
        name="forward",
    )(links, sink, rows)


def backward(links, rows, grads, attended, weights, sink_weight, scaling, slots):
    peers, tokens, _ = grads.shape
    per_device = tokens // BLOCK
    blocks = peers * per_device
    return pl.pallas_call(
        functools.partial(backward_kernel, blocks, slots, per_device, scaling),
        out_shape=(
            jax.ShapeDtypeStruct((peers, 3 * tokens, HEAD), BF16),
            jax.ShapeDtypeStruct((8, BLOCK), F32),
        ),
        in_specs=[SMEM_WHOLE] + [VMEM_WHOLE] * 5,
        out_specs=(VMEM_WHOLE, VMEM_WHOLE),
        scratch_shapes=[
            pltpu.VMEM((blocks, HEAD, BLOCK), BF16),
            pltpu.VMEM((slots * BLOCK, BLOCK), BF16),
            pltpu.VMEM((blocks, BLOCK, HEAD), F32),
            pltpu.VMEM((blocks, BLOCK, HEAD), F32),
        ],
        compiler_params=pltpu.CompilerParams(vmem_limit_bytes=40 << 20),
        cost_estimate=pl.CostEstimate(
            flops=8 * blocks * slots * BLOCK * BLOCK * HEAD,
            bytes_accessed=16 << 20,
            transcendentals=0,
        ),
        name="backward",
    )(links, rows, grads, attended, weights, sink_weight)


def pack_kernel(*refs):
    *sources, out = refs
    tokens = sources[0].shape[1]
    for part, source in enumerate(sources):
        for h in range(out.shape[0]):
            out[h, pl.ds(part * tokens, tokens), :] = source[0, :, pl.ds(h * HEAD, HEAD)]


def unpack_kernel(source, *outs):
    tokens = outs[0].shape[1]
    for part, out in enumerate(outs):
        for h in range(source.shape[0]):
            out[0, :, pl.ds(h * HEAD, HEAD)] = source[h, pl.ds(part * tokens, tokens), :]


def relayout_specs(tokens, count, group):
    flat = pl.BlockSpec((1, tokens, group * HEAD), lambda i: (0, 0, i))
    split = pl.BlockSpec((group, count * tokens, HEAD), lambda i: (i, 0, 0))
    return flat, split


def pack(*arrays, group=4):
    _, tokens, columns = arrays[0].shape
    heads = columns // HEAD
    count = len(arrays)
    flat, split = relayout_specs(tokens, count, group)
    return pl.pallas_call(
        pack_kernel,
        grid=(heads // group,),
        out_shape=jax.ShapeDtypeStruct((heads, count * tokens, HEAD), arrays[0].dtype),
        in_specs=[flat] * count,
        out_specs=split,
        cost_estimate=pl.CostEstimate(
            flops=0, bytes_accessed=4 * count * tokens * columns, transcendentals=0),
        name="pack",
    )(*arrays)


def unpack(array, count, group=4):
    heads, depth, _ = array.shape
    tokens = depth // count
    flat, split = relayout_specs(tokens, count, group)
    return pl.pallas_call(
        unpack_kernel,
        grid=(heads // group,),
        out_shape=(jax.ShapeDtypeStruct((1, tokens, heads * HEAD), array.dtype),) * count,
        in_specs=[split],
        out_specs=(flat,) * count,
        cost_estimate=pl.CostEstimate(
            flops=0, bytes_accessed=4 * heads * depth * HEAD, transcendentals=0),
        name="unpack",
    )(array)


def exchange(array):
    return lax.all_to_all(array, "seq", split_axis=0, concat_axis=0, tiled=True)


def sum_everywhere(values):
    for axis in ("dp", "seq"):
        size = lax.axis_size(axis)
        step = 1
        while step < size:
            pairs = [(i, i ^ step) for i in range(size)]
            values = values + lax.ppermute(values, axis, pairs)
            step *= 2
    return values


def on_device(query_rows, key_rows, value_rows, sink_logit, grad_out, pattern):
    heads, blocks, slots = pattern.shape
    head = lax.axis_index("seq")
    links = lax.dynamic_index_in_dim(pattern, head, 0, keepdims=False).reshape(blocks * slots)
    sink = lax.dynamic_slice_in_dim(sink_logit, head, 1, 0)
    scaling = HEAD ** -0.5

    rows = exchange(pack(query_rows, key_rows, value_rows))
    grads = exchange(pack(grad_out))
    attended, weights, sink_weight = forward(links, sink, rows, scaling, slots)
    attended_tokens = exchange(attended)
    gradients, sink_terms = backward(
        links, rows, grads, attended, weights, sink_weight, scaling, slots)
    gradient_tokens = exchange(gradients)

    own = (lax.broadcasted_iota(jnp.int32, (heads,), 0) == head).astype(F32)
    grad_sink = sum_everywhere(own * -jnp.sum(sink_terms[0])) / lax.axis_size("dp")
    grad_query, grad_key, grad_value = unpack(gradient_tokens, 3)
    (out,) = unpack(attended_tokens, 1)
    return out, grad_query, grad_key, grad_value, grad_sink


def solution(mesh):
    placed = (
        P("dp", "seq", None),
        P("dp", "seq", None),
        P("dp", "seq", None),
        P(),
        P("dp", "seq", None),
        P(),
    )
    return jax.shard_map(
        on_device,
        mesh=mesh,
        in_specs=placed,
        out_specs=(
            P("dp", "seq", None),
            P("dp", "seq", None),
            P("dp", "seq", None),
            P("dp", "seq", None),
            P(),
        ),
        check_vma=False,
    )
```

```python
import functools

import jax
import jax.numpy as jnp
from jax import lax
from jax.experimental import pallas as pl
from jax.experimental.pallas import tpu as pltpu
from jax.sharding import PartitionSpec as P

HEAD = 128
BLOCK = 128
LOG2E = 1.4426950408889634
EXTRA = 16
VMEM_GRANT = 60 << 20
F32 = jnp.float32
BF16 = jnp.bfloat16

NT = (((1,), (1,)), ((), ()))
NN = (((1,), (0,)), ((), ()))
TN = (((0,), (0,)), ((), ()))
VMEM_WHOLE = pl.BlockSpec(memory_space=pltpu.VMEM)
SMEM_WHOLE = pl.BlockSpec(memory_space=pltpu.SMEM)
IN_PLACE = pl.BlockSpec(memory_space=pl.ANY)


def dot(left, right, dims):
    return lax.dot_general(left, right, dims, preferred_element_type=F32)


def tile(ref, block, part, per_device):
    rows = per_device * BLOCK
    half = lax.rem(block, per_device)
    start = pl.multiple_of(part * rows + half * BLOCK, BLOCK)
    return ref.at[lax.div(block, per_device), pl.ds(start, BLOCK), :]


def forward_kernel(blocks, slots, per_device, scaling, links, sink, rows, out, weights, sink_weight,
                   score, weight, result, weight_sem, result_sem):
    sink_value = sink[0]
    chunks = weight_sem.shape[0]
    chunk = blocks // chunks

    def send_weight(i):
        span = pl.ds(i * chunk, chunk)
        return pltpu.make_async_copy(weight.at[span], weights.at[span], weight_sem.at[i])

    def scores_of(b, held):
        queries = tile(rows, b, 0, per_device)[...]
        top = None
        for j in range(slots):
            keys = tile(rows, links[b * slots + j], 1, per_device)[...]
            part = dot(keys, queries, NT)
            held[pl.ds(j * BLOCK, BLOCK), :] = part
            part_top = jnp.max(part, axis=0, keepdims=True)
            top = part_top if top is None else jnp.maximum(top, part_top)
        return jnp.maximum(top * scaling, sink_value)

    def attend(b):
        values = jnp.concatenate(
            [tile(rows, links[b * slots + j], 2, per_device)[...] for j in range(slots)], axis=0)
        tile(result, b, 0, per_device)[...] = dot(weight[b], values, TN).astype(BF16)

    def softmax(b, top, held):
        shift = top * LOG2E
        sink_part = jnp.exp(sink_value - top)
        total = sink_part
        for j in range(slots):
            part = jnp.exp2(held[pl.ds(j * BLOCK, BLOCK), :] * (scaling * LOG2E) - shift)
            held[pl.ds(j * BLOCK, BLOCK), :] = part
            total = total + jnp.sum(part, axis=0, keepdims=True)
        inverse = 1.0 / total
        for j in range(slots):
            weight[b, pl.ds(j * BLOCK, BLOCK), :] = (
                held[pl.ds(j * BLOCK, BLOCK), :] * inverse).astype(BF16)
        sink_weight[pl.ds(b, 1), :] = sink_part * inverse

    def step(b, top, u):
        top_next = scores_of(jnp.minimum(b + 1, blocks - 1), score.at[1 - u])
        attend(jnp.maximum(b - 1, 0))
        softmax(b, top, score.at[u])
        return top_next

    def pair(i, top):
        return step(2 * i + 1, step(2 * i, top, 0), 1)

    def one_chunk(i, top):
        half = chunk // 2
        top = lax.fori_loop(i * half, (i + 1) * half, pair, top)
        send_weight(i).start()
        return top

    weight[0] = jnp.zeros(weight.shape[1:], BF16)
    lax.fori_loop(0, chunks, one_chunk, scores_of(0, score.at[0]))
    attend(blocks - 1)
    send_result = pltpu.make_async_copy(result, out.at[:, pl.ds(0, result.shape[1]), :], result_sem)
    send_result.start()
    for i in range(chunks):
        send_weight(i).wait()
    send_result.wait()


def row_dot_kernel(blocks, per_device, grads_in, attended_in, sink_weight, out, row_dot, grads,
                   attended, terms, load_sem, send_sem):
    tokens = grads.shape[1]
    own = attended_in.at[:, pl.ds(0, tokens), :]
    loads = [
        pltpu.make_async_copy(grads_in, grads, load_sem.at[0]),
        pltpu.make_async_copy(own, attended, load_sem.at[1]),
    ]
    for load in loads:
        load.start()
    for load in loads:
        load.wait()

    def one_block(b, carry):
        grad = tile(grads, b, 0, per_device)[...].astype(F32)
        product = grad * tile(attended, b, 0, per_device)[...].astype(F32)
        row_dot[pl.ds(b, 1), :] = jnp.sum(product.T, axis=0, keepdims=True)
        return carry

    lax.fori_loop(0, blocks, one_block, 0, unroll=4)
    rest = -jnp.sum(sink_weight[...] * row_dot[...], keepdims=True)
    row = lax.broadcasted_iota(jnp.int32, terms.shape[1:], 0)
    stacked = jnp.zeros(terms.shape[1:], F32)
    for i in range(3):
        addend = rest.astype(BF16).astype(F32)
        stacked = jnp.where(row == i, addend, stacked)
        rest = rest - addend
    terms[...] = jnp.broadcast_to(stacked.astype(BF16)[None], terms.shape)
    send = pltpu.make_async_copy(
        terms, out.at[:, pl.ds(tokens, terms.shape[1]), :], send_sem)
    send.start()
    send.wait()


def backward_kernel(blocks, slots, per_device, scaling, links, rows, grads_in, weights, row_dot,
                    out, change, key_sum, value_sum, grads, weight, ready, weight_sem, load_sem,
                    send_sem):
    load = pltpu.make_async_copy(grads_in, grads, load_sem)
    load.start()
    chunks = weight_sem.shape[0]
    chunk = blocks // chunks

    def fetch(i):
        span = pl.ds(i * chunk, chunk)
        return pltpu.make_async_copy(weights.at[span], weight.at[span], weight_sem.at[i])

    for i in range(chunks):
        fetch(i).start()

    def prepare(c, carry):
        key_sum[c] = jnp.zeros((BLOCK, HEAD), F32)
        value_sum[c] = jnp.zeros((BLOCK, HEAD), F32)
        return carry

    lax.fori_loop(0, blocks, prepare, 0)
    load.wait()

    def score_grads(b, j, dots, held):
        values = tile(rows, links[b * slots + j], 2, per_device)[...]
        grad_weight = dot(values, tile(grads, b, 0, per_device)[...], NT)
        part = weight[b, pl.ds(j * BLOCK, BLOCK), :].astype(F32)
        held[pl.ds(j * BLOCK, BLOCK), :] = (part * (grad_weight - dots)).astype(BF16)

    def collect(b, j, held):
        c = links[b * slots + j]
        value_sum[c] += dot(
            weight[b, pl.ds(j * BLOCK, BLOCK), :], tile(grads, b, 0, per_device)[...], NN)
        key_sum[c] += dot(
            held[pl.ds(j * BLOCK, BLOCK), :], tile(rows, b, 0, per_device)[...], NN)

    def query_grad(b, held):
        keys = jnp.concatenate(
            [tile(rows, links[b * slots + j], 1, per_device)[...] for j in range(slots)], axis=0)
        tile(ready, b, 0, per_device)[...] = (dot(held[...], keys, TN) * scaling).astype(BF16)

    def step(b, u):
        ahead = jnp.minimum(b + 1, blocks - 1)
        dots = row_dot[pl.ds(ahead, 1), :]
        for j in range(slots):
            score_grads(ahead, j, dots, change.at[1 - u])
            collect(b, j, change.at[u])
        query_grad(b, change.at[u])

    def pair(i, carry):
        step(2 * i, 0)
        step(2 * i + 1, 1)
        return carry

    fetch(0).wait()
    for j in range(slots):
        score_grads(0, j, row_dot[pl.ds(0, 1), :], change.at[0])

    def one_chunk(i, carry):
        @pl.when(i + 1 < chunks)
        def _():
            fetch(i + 1).wait()

        half = chunk // 2
        return lax.fori_loop(i * half, (i + 1) * half, pair, carry)

    lax.fori_loop(0, chunks, one_chunk, 0)

    def finish(c, carry):
        tile(ready, c, 1, per_device)[...] = (key_sum[c] * scaling).astype(BF16)
        tile(ready, c, 2, per_device)[...] = value_sum[c].astype(BF16)
        return carry

    lax.fori_loop(0, blocks, finish, 0, unroll=2)
    send = pltpu.make_async_copy(ready, out, send_sem)
    send.start()
    send.wait()


def forward(links, sink, rows, scaling, slots):
    peers, depth, _ = rows.shape
    tokens = depth // 3
    per_device = tokens // BLOCK
    blocks = peers * per_device
    return pl.pallas_call(
        functools.partial(forward_kernel, blocks, slots, per_device, scaling),
        out_shape=(
            jax.ShapeDtypeStruct((peers, tokens + EXTRA, HEAD), BF16),
            jax.ShapeDtypeStruct((blocks, slots * BLOCK, BLOCK), BF16),
            jax.ShapeDtypeStruct((blocks, BLOCK), F32),
        ),
        in_specs=[SMEM_WHOLE, SMEM_WHOLE, VMEM_WHOLE],
        out_specs=(IN_PLACE, IN_PLACE, VMEM_WHOLE),
        scratch_shapes=[
            pltpu.VMEM((2, slots * BLOCK, BLOCK), F32),
            pltpu.VMEM((blocks, slots * BLOCK, BLOCK), BF16),
            pltpu.VMEM((peers, tokens, HEAD), BF16),
            pltpu.SemaphoreType.DMA((4,)),
            pltpu.SemaphoreType.DMA,
        ],
        compiler_params=pltpu.CompilerParams(vmem_limit_bytes=VMEM_GRANT),
        cost_estimate=pl.CostEstimate(
            flops=4 * blocks * slots * BLOCK * BLOCK * HEAD,
            bytes_accessed=14 << 20,
            transcendentals=blocks * slots * BLOCK * BLOCK,
        ),
        name="forward",
    )(links, sink, rows)


def row_dots(grads, attended, sink_weight):
    peers, tokens, _ = grads.shape
    per_device = tokens // BLOCK
    blocks = peers * per_device
    return pl.pallas_call(
        functools.partial(row_dot_kernel, blocks, per_device),
        out_shape=(
            jax.ShapeDtypeStruct(attended.shape, BF16),
            jax.ShapeDtypeStruct((blocks, BLOCK), F32),
        ),
        in_specs=[IN_PLACE, IN_PLACE, VMEM_WHOLE],
        out_specs=(IN_PLACE, VMEM_WHOLE),
        scratch_shapes=[
            pltpu.VMEM((peers, tokens, HEAD), BF16),
            pltpu.VMEM((peers, tokens, HEAD), BF16),
            pltpu.VMEM((peers, EXTRA, HEAD), BF16),
            pltpu.SemaphoreType.DMA((2,)),
            pltpu.SemaphoreType.DMA,
        ],
        input_output_aliases={1: 0},
        compiler_params=pltpu.CompilerParams(vmem_limit_bytes=VMEM_GRANT),
        cost_estimate=pl.CostEstimate(
            flops=3 * blocks * BLOCK * HEAD, bytes_accessed=2 << 20, transcendentals=0),
        name="row_dots",
    )(grads, attended, sink_weight)


def backward(links, rows, grads, weights, row_dot, scaling, slots):
    peers, tokens, _ = grads.shape
    per_device = tokens // BLOCK
    blocks = peers * per_device
    return pl.pallas_call(
        functools.partial(backward_kernel, blocks, slots, per_device, scaling),
        out_shape=jax.ShapeDtypeStruct((peers, 3 * tokens, HEAD), BF16),
        in_specs=[SMEM_WHOLE, VMEM_WHOLE, IN_PLACE, IN_PLACE, VMEM_WHOLE],
        out_specs=IN_PLACE,
        scratch_shapes=[
            pltpu.VMEM((2, slots * BLOCK, BLOCK), BF16),
            pltpu.VMEM((blocks, BLOCK, HEAD), F32),
            pltpu.VMEM((blocks, BLOCK, HEAD), F32),
            pltpu.VMEM((peers, tokens, HEAD), BF16),
            pltpu.VMEM((blocks, slots * BLOCK, BLOCK), BF16),
            pltpu.VMEM((peers, 3 * tokens, HEAD), BF16),
            pltpu.SemaphoreType.DMA((4,)),
            pltpu.SemaphoreType.DMA,
            pltpu.SemaphoreType.DMA,
        ],
        compiler_params=pltpu.CompilerParams(vmem_limit_bytes=VMEM_GRANT),
        cost_estimate=pl.CostEstimate(
            flops=8 * blocks * slots * BLOCK * BLOCK * HEAD,
            bytes_accessed=16 << 20,
            transcendentals=0,
        ),
        name="backward",
    )(links, rows, grads, weights, row_dot)


def pack_kernel(*refs):
    *sources, out, flat, split, load_sem, send_sem = refs
    heads, tokens = split.shape[1], split.shape[2]
    loads, sends = [], []
    for part, source in enumerate(sources):
        loads.append(pltpu.make_async_copy(source.at[0], flat.at[part], load_sem.at[part]))
        span = out.at[:, pl.ds(part * tokens, tokens), :]
        sends.append(pltpu.make_async_copy(split.at[part], span, send_sem.at[part]))
        loads[part].start()
    for part in range(len(sources)):
        loads[part].wait()
        for h in range(heads):
            split[part, h] = flat[part, :, pl.ds(h * HEAD, HEAD)]
        sends[part].start()
    for send in sends:
        send.wait()


def pack(*arrays):
    _, tokens, columns = arrays[0].shape
    heads, count = columns // HEAD, len(arrays)
    return pl.pallas_call(
        pack_kernel,
        out_shape=jax.ShapeDtypeStruct((heads, count * tokens, HEAD), arrays[0].dtype),
        in_specs=[IN_PLACE] * count,
        out_specs=IN_PLACE,
        scratch_shapes=[
            pltpu.VMEM((count, tokens, columns), arrays[0].dtype),
            pltpu.VMEM((count, heads, tokens, HEAD), arrays[0].dtype),
            pltpu.SemaphoreType.DMA((count,)),
            pltpu.SemaphoreType.DMA((count,)),
        ],
        compiler_params=pltpu.CompilerParams(vmem_limit_bytes=VMEM_GRANT),
        cost_estimate=pl.CostEstimate(
            flops=0, bytes_accessed=4 * count * tokens * columns, transcendentals=0),
        name="pack",
    )(*arrays)


def unpack_kernel(source, *refs):
    *outs, flat, send_sem = refs
    heads, tokens = source.shape[0], flat.shape[1]
    sends = []
    for part, out in enumerate(outs):
        for h in range(heads):
            flat[part, :, pl.ds(h * HEAD, HEAD)] = source[h, pl.ds(part * tokens, tokens), :]
        sends.append(pltpu.make_async_copy(flat.at[part], out.at[0], send_sem.at[part]))
        sends[part].start()
    for send in sends:
        send.wait()


def unpack(array, tokens, count, grant):
    heads = array.shape[0]
    return pl.pallas_call(
        unpack_kernel,
        out_shape=(jax.ShapeDtypeStruct((1, tokens, heads * HEAD), array.dtype),) * count,
        in_specs=[VMEM_WHOLE],
        out_specs=(IN_PLACE,) * count,
        scratch_shapes=[
            pltpu.VMEM((count, tokens, heads * HEAD), array.dtype),
            pltpu.SemaphoreType.DMA((count,)),
        ],
        compiler_params=pltpu.CompilerParams(vmem_limit_bytes=grant),
        cost_estimate=pl.CostEstimate(
            flops=0, bytes_accessed=4 * heads * count * tokens * HEAD, transcendentals=0),
        name="unpack",
    )(array)


def exchange(array):
    return lax.all_to_all(array, "seq", split_axis=0, concat_axis=0, tiled=True)


def sum_over_documents(values):
    size = lax.axis_size("dp")
    stride = 1
    while stride < size:
        width = min(4, size // stride)
        shifted = []
        for k in range(1, width):
            pairs = []
            for i in range(size):
                digit = i // stride % width
                pairs.append((i, i + ((digit + k) % width - digit) * stride))
            shifted.append(lax.ppermute(values, "dp", pairs))
        values = functools.reduce(jnp.add, shifted, values)
        stride *= width
    return values


def on_device(query_rows, key_rows, value_rows, sink_logit, grad_out, pattern):
    heads, blocks, slots = pattern.shape
    head = lax.axis_index("seq")
    links = lax.dynamic_index_in_dim(pattern, head, 0, keepdims=False).reshape(blocks * slots)
    sink = lax.dynamic_slice_in_dim(sink_logit, head, 1, 0)
    scaling = HEAD ** -0.5

    tokens = query_rows.shape[1]
    rows = exchange(pack(query_rows, key_rows, value_rows))
    grads = exchange(pack(grad_out))
    attended, weights, sink_weight = forward(links, sink, rows, scaling, slots)
    attended, row_dot = row_dots(grads, attended, sink_weight)
    attended_tokens = exchange(attended)
    gradients = backward(links, rows, grads, weights, row_dot, scaling, slots)
    gradient_tokens = exchange(gradients)

    addends = attended_tokens[:, tokens:tokens + 3, 0].astype(F32)
    grad_sink = sum_over_documents(jnp.sum(addends, axis=1)) / lax.axis_size("dp")
    (out,) = unpack(attended_tokens, tokens, 1, VMEM_GRANT)
    grad_query, grad_key, grad_value = unpack(gradient_tokens, tokens, 3, 8 << 20)
    return out, grad_query, grad_key, grad_value, grad_sink


def solution(mesh):
    placed = (
        P("dp", "seq", None),
        P("dp", "seq", None),
        P("dp", "seq", None),
        P(),
        P("dp", "seq", None),
        P(),
    )
    return jax.shard_map(
        on_device,
        mesh=mesh,
        in_specs=placed,
        out_specs=(
            P("dp", "seq", None),
            P("dp", "seq", None),
            P("dp", "seq", None),
            P("dp", "seq", None),
            P(),
        ),
        check_vma=False,
    )
```

```python
import functools

import jax
import jax.numpy as jnp
from jax import lax
from jax.experimental import pallas as pl
from jax.experimental.pallas import tpu as pltpu
from jax.sharding import PartitionSpec as P

HEAD = 128
BLOCK = 128
LOG2E = 1.4426950408889634
EXTRA = 16
VMEM_GRANT = 63 << 20
F32 = jnp.float32
BF16 = jnp.bfloat16

NT = (((1,), (1,)), ((), ()))
NN = (((1,), (0,)), ((), ()))
TN = (((0,), (0,)), ((), ()))
VMEM_WHOLE = pl.BlockSpec(memory_space=pltpu.VMEM)
SMEM_WHOLE = pl.BlockSpec(memory_space=pltpu.SMEM)
IN_PLACE = pl.BlockSpec(memory_space=pl.ANY)


def dot(left, right, dims):
    return lax.dot_general(left, right, dims, preferred_element_type=F32)


def tile(ref, block, part, per_device):
    rows = per_device * BLOCK
    half = lax.rem(block, per_device)
    start = pl.multiple_of(part * rows + half * BLOCK, BLOCK)
    return ref.at[lax.div(block, per_device), pl.ds(start, BLOCK), :]


def forward_kernel(blocks, slots, per_device, scaling, links, sink, rows_in, out, weights,
                   sink_weight, score, rows, weight, result, load_sem, weight_sem, result_sem):
    sink_value = sink[0]
    tokens = result.shape[1]
    loads = []
    for k, span in enumerate((pl.ds(0, 2 * tokens), pl.ds(2 * tokens, tokens))):
        loads.append(pltpu.make_async_copy(
            rows_in.at[:, span, :], rows.at[:, span, :], load_sem.at[k]))
        loads[k].start()
    chunks = weight_sem.shape[0]
    chunk = blocks // chunks
    unroll = score.shape[0]

    def send_weight(i):
        span = pl.ds(i * chunk, chunk)
        return pltpu.make_async_copy(weight.at[span], weights.at[span], weight_sem.at[i])

    def scores_of(b, held):
        queries = tile(rows, b, 0, per_device)[...]
        keys = jnp.concatenate(
            [tile(rows, links[b * slots + j], 1, per_device)[...] for j in range(slots)], axis=0)
        whole = dot(keys, queries, NT)
        held[...] = whole
        top = None
        for j in range(slots):
            part = whole[j * BLOCK:(j + 1) * BLOCK]
            part_top = jnp.max(part.reshape(-1, 8, BLOCK), axis=0)
            top = part_top if top is None else jnp.maximum(top, part_top)
        return jnp.maximum(jnp.max(top, axis=0, keepdims=True) * scaling, sink_value)

    def attend(b):
        values = jnp.concatenate(
            [tile(rows, links[b * slots + j], 2, per_device)[...] for j in range(slots)], axis=0)
        tile(result, b, 0, per_device)[...] = dot(weight[b], values, TN).astype(BF16)

    def softmax(b, top, held):
        shift = top * LOG2E
        sink_part = jnp.exp(sink_value - top)
        total = None
        for j in range(slots):
            part = jnp.exp2(held[pl.ds(j * BLOCK, BLOCK), :] * (scaling * LOG2E) - shift)
            held[pl.ds(j * BLOCK, BLOCK), :] = part
            part_total = jnp.sum(part.reshape(-1, 8, BLOCK), axis=0)
            total = part_total if total is None else total + part_total
        inverse = 1.0 / (sink_part + jnp.sum(total, axis=0, keepdims=True))
        for j in range(slots):
            weight[b, pl.ds(j * BLOCK, BLOCK), :] = (
                held[pl.ds(j * BLOCK, BLOCK), :] * inverse).astype(BF16)
        sink_weight[pl.ds(b, 1), :] = sink_part * inverse

    def step(b, top, u):
        top_next = scores_of(jnp.minimum(b + 1, blocks - 1), score.at[(u + 1) % unroll])
        attend(jnp.maximum(b - 1, 0))
        softmax(b, top, score.at[u])
        return top_next

    def several(i, top):
        for u in range(unroll):
            top = step(unroll * i + u, top, u)
        return top

    def one_chunk(i, top):
        trips = chunk // unroll
        top = lax.fori_loop(i * trips, (i + 1) * trips, several, top)
        send_weight(i).start()
        return top

    weight[0] = jnp.zeros(weight.shape[1:], BF16)
    loads[0].wait()
    top = scores_of(0, score.at[0])
    loads[1].wait()
    lax.fori_loop(0, chunks, one_chunk, top)
    attend(blocks - 1)
    send_result = pltpu.make_async_copy(result, out, result_sem)
    send_result.start()
    for i in range(chunks):
        send_weight(i).wait()
    send_result.wait()


def value_kernel(blocks, slots, per_device, links, grads_in, attended_in, weights, sink_weight, out,
                 row_dot, grads, attended, weight, value_sum, ready, load_sem, send_sem):
    tokens = grads.shape[1]
    chunks = load_sem.shape[1]
    chunk = blocks // chunks

    def fetch(i):
        peers = pl.ds(i * (chunk // per_device), chunk // per_device)
        span = pl.ds(i * chunk, chunk)
        return (
            pltpu.make_async_copy(grads_in.at[peers], grads.at[peers], load_sem.at[0, i]),
            pltpu.make_async_copy(attended_in.at[peers], attended.at[peers], load_sem.at[1, i]),
            pltpu.make_async_copy(weights.at[span], weight.at[span], load_sem.at[2, i]),
        )

    for i in range(2):
        for load in fetch(i):
            load.start()

    def prepare(c, carry):
        value_sum[c] = jnp.zeros((BLOCK, HEAD), F32)
        return carry

    lax.fori_loop(0, blocks, prepare, 0, unroll=4)

    def one_block(b):
        grad = tile(grads, b, 0, per_device)[...]
        parts = dot(weight[b], grad, NN)
        product = grad.astype(F32) * tile(attended, b, 0, per_device)[...].astype(F32)
        row_dot[pl.ds(b, 1), :] = jnp.sum(product.T, axis=0, keepdims=True)
        for j in range(slots):
            value_sum[links[b * slots + j]] += parts[j * BLOCK:(j + 1) * BLOCK]

    def one_chunk(i, carry):
        @pl.when(i + 2 < chunks)
        def _():
            for load in fetch(i + 2):
                load.start()

        for load in fetch(i):
            load.wait()
        for u in range(chunk):
            one_block(i * chunk + u)
        return carry

    lax.fori_loop(0, chunks, one_chunk, 0)

    def finish(c, carry):
        tile(ready, c, 0, per_device)[...] = value_sum[c].astype(BF16)
        return carry

    lax.fori_loop(0, blocks, finish, 0, unroll=4)
    rest = -jnp.sum(sink_weight[...] * row_dot[...], keepdims=True)
    row = lax.broadcasted_iota(jnp.int32, (EXTRA, HEAD), 0)
    stacked = jnp.zeros((EXTRA, HEAD), F32)
    for i in range(3):
        addend = rest.astype(BF16).astype(F32)
        stacked = jnp.where(row == i, addend, stacked)
        rest = rest - addend
    ready[:, pl.ds(tokens, EXTRA), :] = jnp.broadcast_to(
        stacked.astype(BF16)[None], (ready.shape[0], EXTRA, HEAD))
    send = pltpu.make_async_copy(ready, out, send_sem)
    send.start()
    send.wait()


def backward_kernel(blocks, slots, per_device, scaling, links, rows_in, grads_in, weights, row_dot,
                    out, change, key_sum, rows, grads, weight, ready, weight_sem, load_sem, send_sem):
    tokens = grads.shape[1]
    chunks = weight_sem.shape[0]
    chunk = blocks // chunks
    unroll = change.shape[0]
    values_at = pl.ds(2 * tokens, tokens)
    others_at = pl.ds(0, 2 * tokens)
    loads = [
        pltpu.make_async_copy(grads_in, grads, load_sem.at[0]),
        pltpu.make_async_copy(rows_in.at[:, values_at, :], rows.at[:, values_at, :], load_sem.at[1]),
        pltpu.make_async_copy(rows_in.at[:, others_at, :], rows.at[:, others_at, :], load_sem.at[2]),
    ]

    def fetch(i):
        span = pl.ds(i * chunk, chunk)
        return pltpu.make_async_copy(weights.at[span], weight.at[span], weight_sem.at[i])

    loads[0].start()
    loads[1].start()
    fetch(0).start()
    loads[2].start()
    fetch(1).start()

    def prepare(c, carry):
        key_sum[c] = jnp.zeros((BLOCK, HEAD), F32)
        return carry

    lax.fori_loop(0, blocks, prepare, 0, unroll=4)

    def score_grads(b, held):
        values = jnp.concatenate(
            [tile(rows, links[b * slots + j], 2, per_device)[...] for j in range(slots)], axis=0)
        grad_weight = dot(values, tile(grads, b, 0, per_device)[...], NT)
        dots = row_dot[pl.ds(b, 1), :]
        held[...] = (weight[b].astype(F32) * (grad_weight - dots)).astype(BF16)

    def collect(b, held):
        parts = dot(held[...], tile(rows, b, 0, per_device)[...], NN)
        for j in range(slots):
            key_sum[links[b * slots + j]] += parts[j * BLOCK:(j + 1) * BLOCK]

    def query_grad(b, held):
        keys = jnp.concatenate(
            [tile(rows, links[b * slots + j], 1, per_device)[...] for j in range(slots)], axis=0)
        tile(ready, b, 0, per_device)[...] = (dot(held[...], keys, TN) * scaling).astype(BF16)

    def several(i, carry):
        for u in range(unroll):
            b = unroll * i + u
            score_grads(jnp.minimum(b + 1, blocks - 1), change.at[(u + 1) % unroll])
            collect(b, change.at[u])
            query_grad(b, change.at[u])
        return carry

    for load in loads[:2]:
        load.wait()
    fetch(0).wait()
    score_grads(0, change.at[0])
    loads[2].wait()

    def one_chunk(i, carry):
        @pl.when(i + 2 < chunks)
        def _():
            fetch(i + 2).start()

        @pl.when(i + 1 < chunks)
        def _():
            fetch(i + 1).wait()

        trips = chunk // unroll
        return lax.fori_loop(i * trips, (i + 1) * trips, several, carry)

    lax.fori_loop(0, chunks, one_chunk, 0)

    def finish(c, carry):
        tile(ready, c, 1, per_device)[...] = (key_sum[c] * scaling).astype(BF16)
        return carry

    lax.fori_loop(0, blocks, finish, 0, unroll=4)
    send = pltpu.make_async_copy(ready, out, send_sem)
    send.start()
    send.wait()


def forward(links, sink, rows, scaling, slots):
    peers, depth, _ = rows.shape
    tokens = depth // 3
    per_device = tokens // BLOCK
    blocks = peers * per_device
    return pl.pallas_call(
        functools.partial(forward_kernel, blocks, slots, per_device, scaling),
        out_shape=(
            jax.ShapeDtypeStruct((peers, tokens, HEAD), BF16),
            jax.ShapeDtypeStruct((blocks, slots * BLOCK, BLOCK), BF16),
            jax.ShapeDtypeStruct((blocks, BLOCK), F32),
        ),
        in_specs=[SMEM_WHOLE, SMEM_WHOLE, IN_PLACE],
        out_specs=(IN_PLACE, IN_PLACE, VMEM_WHOLE),
        scratch_shapes=[
            pltpu.VMEM((8, slots * BLOCK, BLOCK), F32),
            pltpu.VMEM(rows.shape, BF16),
            pltpu.VMEM((blocks, slots * BLOCK, BLOCK), BF16),
            pltpu.VMEM((peers, tokens, HEAD), BF16),
            pltpu.SemaphoreType.DMA((2,)),
            pltpu.SemaphoreType.DMA((4,)),
            pltpu.SemaphoreType.DMA,
        ],
        compiler_params=pltpu.CompilerParams(vmem_limit_bytes=VMEM_GRANT),
        cost_estimate=pl.CostEstimate(
            flops=4 * blocks * slots * BLOCK * BLOCK * HEAD,
            bytes_accessed=14 << 20,
            transcendentals=blocks * slots * BLOCK * BLOCK,
        ),
        name="forward",
    )(links, sink, rows)


def value_grad(links, grads, attended, weights, sink_weight):
    peers, tokens, _ = grads.shape
    per_device = tokens // BLOCK
    blocks = peers * per_device
    slots = weights.shape[1] // BLOCK
    return pl.pallas_call(
        functools.partial(value_kernel, blocks, slots, per_device),
        out_shape=(
            jax.ShapeDtypeStruct((peers, tokens + EXTRA, HEAD), BF16),
            jax.ShapeDtypeStruct((blocks, BLOCK), F32),
        ),
        in_specs=[SMEM_WHOLE, IN_PLACE, IN_PLACE, IN_PLACE, VMEM_WHOLE],
        out_specs=(IN_PLACE, VMEM_WHOLE),
        scratch_shapes=[
            pltpu.VMEM((peers, tokens, HEAD), BF16),
            pltpu.VMEM((peers, tokens, HEAD), BF16),
            pltpu.VMEM(weights.shape, BF16),
            pltpu.VMEM((blocks, BLOCK, HEAD), F32),
            pltpu.VMEM((peers, tokens + EXTRA, HEAD), BF16),
            pltpu.SemaphoreType.DMA((3, 4)),
            pltpu.SemaphoreType.DMA,
        ],
        compiler_params=pltpu.CompilerParams(vmem_limit_bytes=VMEM_GRANT),
        cost_estimate=pl.CostEstimate(
            flops=2 * blocks * slots * BLOCK * BLOCK * HEAD,
            bytes_accessed=12 << 20,
            transcendentals=0,
        ),
        name="value_grad",
    )(links, grads, attended, weights, sink_weight)


def backward(links, rows, grads, weights, row_dot, scaling):
    peers, tokens, _ = grads.shape
    per_device = tokens // BLOCK
    blocks = peers * per_device
    slots = weights.shape[1] // BLOCK
    return pl.pallas_call(
        functools.partial(backward_kernel, blocks, slots, per_device, scaling),
        out_shape=jax.ShapeDtypeStruct((peers, 2 * tokens, HEAD), BF16),
        in_specs=[SMEM_WHOLE, IN_PLACE, IN_PLACE, IN_PLACE, VMEM_WHOLE],
        out_specs=IN_PLACE,
        scratch_shapes=[
            pltpu.VMEM((8, slots * BLOCK, BLOCK), BF16),
            pltpu.VMEM((blocks, BLOCK, HEAD), F32),
            pltpu.VMEM(rows.shape, BF16),
            pltpu.VMEM((peers, tokens, HEAD), BF16),
            pltpu.VMEM(weights.shape, BF16),
            pltpu.VMEM((peers, 2 * tokens, HEAD), BF16),
            pltpu.SemaphoreType.DMA((4,)),
            pltpu.SemaphoreType.DMA((3,)),
            pltpu.SemaphoreType.DMA,
        ],
        compiler_params=pltpu.CompilerParams(vmem_limit_bytes=VMEM_GRANT),
        cost_estimate=pl.CostEstimate(
            flops=6 * blocks * slots * BLOCK * BLOCK * HEAD,
            bytes_accessed=16 << 20,
            transcendentals=0,
        ),
        name="backward",
    )(links, rows, grads, weights, row_dot)


def pack_kernel(*refs):
    *sources, out, flat, split, load_sem, send_sem = refs
    heads, tokens = split.shape[1], split.shape[2]
    loads, sends = [], []
    for part, source in enumerate(sources):
        loads.append(pltpu.make_async_copy(source.at[0], flat.at[part], load_sem.at[part]))
        span = out.at[:, pl.ds(part * tokens, tokens), :]
        sends.append(pltpu.make_async_copy(split.at[part], span, send_sem.at[part]))
        loads[part].start()
    for part in range(len(sources)):
        loads[part].wait()
        for h in range(heads):
            split[part, h] = flat[part, :, pl.ds(h * HEAD, HEAD)]
        sends[part].start()
    for send in sends:
        send.wait()


def pack(*arrays):
    _, tokens, columns = arrays[0].shape
    heads, count = columns // HEAD, len(arrays)
    return pl.pallas_call(
        pack_kernel,
        out_shape=jax.ShapeDtypeStruct((heads, count * tokens, HEAD), arrays[0].dtype),
        in_specs=[IN_PLACE] * count,
        out_specs=IN_PLACE,
        scratch_shapes=[
            pltpu.VMEM((count, tokens, columns), arrays[0].dtype),
            pltpu.VMEM((count, heads, tokens, HEAD), arrays[0].dtype),
            pltpu.SemaphoreType.DMA((count,)),
            pltpu.SemaphoreType.DMA((count,)),
        ],
        compiler_params=pltpu.CompilerParams(vmem_limit_bytes=VMEM_GRANT),
        cost_estimate=pl.CostEstimate(
            flops=0, bytes_accessed=4 * count * tokens * columns, transcendentals=0),
        name="pack",
    )(*arrays)


def unpack_kernel(source, *refs):
    *outs, split, flat, load_sem, send_sem = refs
    heads, tokens = source.shape[0], flat.shape[1]
    loads, sends = [], []
    for part, out in enumerate(outs):
        span = source.at[:, pl.ds(part * tokens, tokens), :]
        loads.append(pltpu.make_async_copy(span, split.at[part], load_sem.at[part]))
        sends.append(pltpu.make_async_copy(flat.at[part], out.at[0], send_sem.at[part]))
        loads[part].start()
    for part in range(len(outs)):
        loads[part].wait()
        for h in range(heads):
            flat[part, :, pl.ds(h * HEAD, HEAD)] = split[part, h]
        sends[part].start()
    for send in sends:
        send.wait()


def unpack(array, tokens, count):
    heads = array.shape[0]
    return pl.pallas_call(
        unpack_kernel,
        out_shape=(jax.ShapeDtypeStruct((1, tokens, heads * HEAD), array.dtype),) * count,
        in_specs=[IN_PLACE],
        out_specs=(IN_PLACE,) * count,
        scratch_shapes=[
            pltpu.VMEM((count, heads, tokens, HEAD), array.dtype),
            pltpu.VMEM((count, tokens, heads * HEAD), array.dtype),
            pltpu.SemaphoreType.DMA((count,)),
            pltpu.SemaphoreType.DMA((count,)),
        ],
        compiler_params=pltpu.CompilerParams(vmem_limit_bytes=VMEM_GRANT),
        cost_estimate=pl.CostEstimate(
            flops=0, bytes_accessed=4 * heads * count * tokens * HEAD, transcendentals=0),
        name="unpack",
    )(array)


def exchange(array):
    return lax.all_to_all(array, "seq", split_axis=0, concat_axis=0, tiled=True)


def sum_over_documents(values):
    size = lax.axis_size("dp")
    stride = 1
    while stride < size:
        width = min(4, size // stride)
        shifted = []
        for k in range(1, width):
            pairs = []
            for i in range(size):
                digit = i // stride % width
                pairs.append((i, i + ((digit + k) % width - digit) * stride))
            shifted.append(lax.ppermute(values, "dp", pairs))
        values = functools.reduce(jnp.add, shifted, values)
        stride *= width
    return values


def on_device(query_rows, key_rows, value_rows, sink_logit, grad_out, pattern):
    heads, blocks, slots = pattern.shape
    head = lax.axis_index("seq")
    links = lax.dynamic_index_in_dim(pattern, head, 0, keepdims=False).reshape(blocks * slots)
    sink = lax.dynamic_slice_in_dim(sink_logit, head, 1, 0)
    scaling = HEAD ** -0.5

    tokens = query_rows.shape[1]
    grad_out, links, sink = lax.optimization_barrier((grad_out, links, sink))
    rows = exchange(pack(query_rows, key_rows, value_rows))
    grads = exchange(pack(grad_out))
    attended, weights, sink_weight = forward(links, sink, rows, scaling, slots)
    attended_tokens = exchange(attended)
    values, row_dot = value_grad(links, grads, attended, weights, sink_weight)
    attended_tokens, values, row_dot = lax.optimization_barrier((attended_tokens, values, row_dot))
    value_tokens = exchange(values)
    others = backward(links, rows, grads, weights, row_dot, scaling)
    value_tokens, others = lax.optimization_barrier((value_tokens, others))
    other_tokens = exchange(others)

    addends = value_tokens[:, tokens:tokens + 3, 0].astype(F32)
    grad_sink = sum_over_documents(jnp.sum(addends, axis=1)) / lax.axis_size("dp")
    (out,) = unpack(attended_tokens, tokens, 1)
    (grad_value,) = unpack(value_tokens, tokens, 1)
    grad_query, grad_key = unpack(other_tokens, tokens, 2)
    return out, grad_query, grad_key, grad_value, grad_sink


def solution(mesh):
    placed = (
        P("dp", "seq", None),
        P("dp", "seq", None),
        P("dp", "seq", None),
        P(),
        P("dp", "seq", None),
        P(),
    )
    return jax.shard_map(
        on_device,
        mesh=mesh,
        in_specs=placed,
        out_specs=(
            P("dp", "seq", None),
            P("dp", "seq", None),
            P("dp", "seq", None),
            P("dp", "seq", None),
            P(),
        ),
        check_vma=False,
    )
```

```python
import functools

import jax
import jax.numpy as jnp
from jax import lax
from jax.experimental import pallas as pl
from jax.experimental.pallas import tpu as pltpu
from jax.sharding import PartitionSpec as P

HEAD = 128
BLOCK = 128
LOG2E = 1.4426950408889634
EXTRA = 16
VMEM_GRANT = 63 << 20
F32 = jnp.float32
BF16 = jnp.bfloat16

NT = (((1,), (1,)), ((), ()))
NN = (((1,), (0,)), ((), ()))
TN = (((0,), (0,)), ((), ()))
VMEM_WHOLE = pl.BlockSpec(memory_space=pltpu.VMEM)
SMEM_WHOLE = pl.BlockSpec(memory_space=pltpu.SMEM)
IN_PLACE = pl.BlockSpec(memory_space=pl.ANY)


def dot(left, right, dims):
    return lax.dot_general(left, right, dims, preferred_element_type=F32)


def tile(ref, block, part, per_device):
    rows = per_device * BLOCK
    half = lax.rem(block, per_device)
    start = pl.multiple_of(part * rows + half * BLOCK, BLOCK)
    return ref.at[lax.div(block, per_device), pl.ds(start, BLOCK), :]


def forward_kernel(blocks, slots, per_device, scaling, links, sink, rows_in, out, weights,
                   sink_weight, score, rows, weight, result, load_sem, weight_sem, result_sem):
    sink_value = sink[0]
    tokens = result.shape[1]
    loads = []
    for k, span in enumerate((pl.ds(0, 2 * tokens), pl.ds(2 * tokens, tokens))):
        loads.append(pltpu.make_async_copy(
            rows_in.at[:, span, :], rows.at[:, span, :], load_sem.at[k]))
        loads[k].start()
    chunks = weight_sem.shape[0]
    chunk = blocks // chunks
    unroll = score.shape[0]

    def send_weight(i):
        span = pl.ds(i * chunk, chunk)
        return pltpu.make_async_copy(weight.at[span], weights.at[span], weight_sem.at[i])

    def scores_of(b, held):
        queries = tile(rows, b, 0, per_device)[...]
        keys = jnp.concatenate(
            [tile(rows, links[b * slots + j], 1, per_device)[...] for j in range(slots)], axis=0)
        whole = dot(keys, queries, NT)
        held[...] = whole
        top = None
        for j in range(slots):
            part = whole[j * BLOCK:(j + 1) * BLOCK]
            part_top = jnp.max(part.reshape(-1, 8, BLOCK), axis=0)
            top = part_top if top is None else jnp.maximum(top, part_top)
        return jnp.maximum(jnp.max(top, axis=0, keepdims=True) * scaling, sink_value)

    def attend(b):
        values = jnp.concatenate(
            [tile(rows, links[b * slots + j], 2, per_device)[...] for j in range(slots)], axis=0)
        tile(result, b, 0, per_device)[...] = dot(weight[b], values, TN).astype(BF16)

    def softmax(b, top, held):
        shift = top * LOG2E
        sink_part = jnp.exp(sink_value - top)
        total = None
        for j in range(slots):
            part = jnp.exp2(held[pl.ds(j * BLOCK, BLOCK), :] * (scaling * LOG2E) - shift)
            held[pl.ds(j * BLOCK, BLOCK), :] = part
            part_total = jnp.sum(part.reshape(-1, 8, BLOCK), axis=0)
            total = part_total if total is None else total + part_total
        inverse = 1.0 / (sink_part + jnp.sum(total, axis=0, keepdims=True))
        for j in range(slots):
            weight[b, pl.ds(j * BLOCK, BLOCK), :] = (
                held[pl.ds(j * BLOCK, BLOCK), :] * inverse).astype(BF16)
        sink_weight[pl.ds(b, 1), :] = sink_part * inverse

    def step(b, top, u):
        top_next = scores_of(jnp.minimum(b + 1, blocks - 1), score.at[(u + 1) % unroll])
        attend(jnp.maximum(b - 1, 0))
        softmax(b, top, score.at[u])
        return top_next

    def several(i, top):
        for u in range(unroll):
            top = step(unroll * i + u, top, u)
        return top

    def one_chunk(i, top):
        trips = chunk // unroll
        top = lax.fori_loop(i * trips, (i + 1) * trips, several, top)
        send_weight(i).start()
        return top

    weight[0] = jnp.zeros(weight.shape[1:], BF16)
    loads[0].wait()
    top = scores_of(0, score.at[0])
    loads[1].wait()
    lax.fori_loop(0, chunks, one_chunk, top)
    attend(blocks - 1)
    send_result = pltpu.make_async_copy(result, out, result_sem)
    send_result.start()
    for i in range(chunks):
        send_weight(i).wait()
    send_result.wait()


def value_kernel(blocks, slots, per_device, links, rows_in, grads_in, attended_in, weights,
                 sink_weight, out, changes, row_dot, grads, attended, values, weight, change,
                 value_sum, ready, load_sem, value_sem, change_sem, send_sem):
    tokens = grads.shape[1]
    chunks = load_sem.shape[1]
    chunk = blocks // chunks

    def fetch(i):
        peers = pl.ds(i * (chunk // per_device), chunk // per_device)
        span = pl.ds(i * chunk, chunk)
        return (
            pltpu.make_async_copy(grads_in.at[peers], grads.at[peers], load_sem.at[0, i]),
            pltpu.make_async_copy(attended_in.at[peers], attended.at[peers], load_sem.at[1, i]),
            pltpu.make_async_copy(weights.at[span], weight.at[span], load_sem.at[2, i]),
        )

    def send_change(i):
        span = pl.ds(i * chunk, chunk)
        return pltpu.make_async_copy(change.at[span], changes.at[span], change_sem.at[i])

    load_values = pltpu.make_async_copy(
        rows_in.at[:, pl.ds(2 * tokens, tokens), :], values, value_sem)
    load_values.start()
    for i in range(2):
        for load in fetch(i):
            load.start()

    def prepare(c, carry):
        value_sum[c] = jnp.zeros((BLOCK, HEAD), F32)
        return carry

    lax.fori_loop(0, blocks, prepare, 0, unroll=4)

    def dots_of(b):
        product = tile(grads, b, 0, per_device)[...].astype(F32)
        product = product * tile(attended, b, 0, per_device)[...].astype(F32)
        return jnp.sum(product.T, axis=0, keepdims=True)

    def one_block(b, dots):
        grad = tile(grads, b, 0, per_device)[...]
        chosen = [links[b * slots + j] for j in range(slots)]
        picked = jnp.concatenate([tile(values, c, 0, per_device)[...] for c in chosen], axis=0)
        grad_weight = dot(picked, grad, NT)
        parts = dot(weight[b], grad, NN)
        change[b] = (weight[b].astype(F32) * (grad_weight - dots)).astype(BF16)
        for j, c in enumerate(chosen):
            value_sum[c] += parts[j * BLOCK:(j + 1) * BLOCK]

    def one_chunk(i, carry):
        @pl.when(i + 2 < chunks)
        def _():
            for load in fetch(i + 2):
                load.start()

        for load in fetch(i):
            load.wait()
        dots = [dots_of(i * chunk + u) for u in range(chunk)]
        for u in range(chunk):
            row_dot[pl.ds(i * chunk + u, 1), :] = dots[u]
            one_block(i * chunk + u, dots[u])
        send_change(i).start()
        return carry

    load_values.wait()
    lax.fori_loop(0, chunks, one_chunk, 0)

    def finish(c, carry):
        tile(ready, c, 0, per_device)[...] = value_sum[c].astype(BF16)
        return carry

    lax.fori_loop(0, blocks, finish, 0, unroll=4)
    rest = -jnp.sum(sink_weight[...] * row_dot[...], keepdims=True)
    row = lax.broadcasted_iota(jnp.int32, (EXTRA, HEAD), 0)
    stacked = jnp.zeros((EXTRA, HEAD), F32)
    for i in range(3):
        addend = rest.astype(BF16).astype(F32)
        stacked = jnp.where(row == i, addend, stacked)
        rest = rest - addend
    ready[:, pl.ds(tokens, EXTRA), :] = jnp.broadcast_to(
        stacked.astype(BF16)[None], (ready.shape[0], EXTRA, HEAD))
    send = pltpu.make_async_copy(ready, out, send_sem)
    send.start()
    for i in range(chunks):
        send_change(i).wait()
    send.wait()


def backward_kernel(blocks, slots, per_device, scaling, links, rows_in, changes, out, key_sum, rows,
                    change, ready, change_sem, load_sem, send_sem):
    chunks = change_sem.shape[0]
    chunk = blocks // chunks
    load = pltpu.make_async_copy(rows_in.at[:, pl.ds(0, rows.shape[1]), :], rows, load_sem)
    load.start()

    def fetch(i):
        span = pl.ds(i * chunk, chunk)
        return pltpu.make_async_copy(changes.at[span], change.at[span], change_sem.at[i])

    fetch(0).start()
    fetch(1).start()

    def prepare(c, carry):
        key_sum[c] = jnp.zeros((BLOCK, HEAD), F32)
        return carry

    lax.fori_loop(0, blocks, prepare, 0, unroll=4)

    def one_block(b):
        chosen = [links[b * slots + j] for j in range(slots)]
        parts = dot(change[b], tile(rows, b, 0, per_device)[...], NN)
        keys = jnp.concatenate([tile(rows, c, 1, per_device)[...] for c in chosen], axis=0)
        tile(ready, b, 0, per_device)[...] = (dot(change[b], keys, TN) * scaling).astype(BF16)
        for j, c in enumerate(chosen):
            key_sum[c] += parts[j * BLOCK:(j + 1) * BLOCK]

    def one_chunk(i, carry):
        @pl.when(i + 2 < chunks)
        def _():
            fetch(i + 2).start()

        fetch(i).wait()
        for u in range(chunk):
            one_block(i * chunk + u)
        return carry

    load.wait()
    lax.fori_loop(0, chunks, one_chunk, 0)

    pieces = send_sem.shape[0]
    sends = []
    for i in range(pieces):
        for c in range(i * blocks // pieces, (i + 1) * blocks // pieces):
            tile(ready, c, 1, per_device)[...] = (key_sum[c] * scaling).astype(BF16)
        peers = out.shape[0] // pieces
        span = pl.ds(i * peers, peers)
        sends.append(pltpu.make_async_copy(ready.at[span], out.at[span], send_sem.at[i]))
        sends[i].start()
    for send in sends:
        send.wait()


def forward(links, sink, rows, scaling, slots):
    peers, depth, _ = rows.shape
    tokens = depth // 3
    per_device = tokens // BLOCK
    blocks = peers * per_device
    return pl.pallas_call(
        functools.partial(forward_kernel, blocks, slots, per_device, scaling),
        out_shape=(
            jax.ShapeDtypeStruct((peers, tokens, HEAD), BF16),
            jax.ShapeDtypeStruct((blocks, slots * BLOCK, BLOCK), BF16),
            jax.ShapeDtypeStruct((blocks, BLOCK), F32),
        ),
        in_specs=[SMEM_WHOLE, SMEM_WHOLE, IN_PLACE],
        out_specs=(IN_PLACE, IN_PLACE, VMEM_WHOLE),
        scratch_shapes=[
            pltpu.VMEM((8, slots * BLOCK, BLOCK), F32),
            pltpu.VMEM(rows.shape, BF16),
            pltpu.VMEM((blocks, slots * BLOCK, BLOCK), BF16),
            pltpu.VMEM((peers, tokens, HEAD), BF16),
            pltpu.SemaphoreType.DMA((2,)),
            pltpu.SemaphoreType.DMA((4,)),
            pltpu.SemaphoreType.DMA,
        ],
        compiler_params=pltpu.CompilerParams(vmem_limit_bytes=VMEM_GRANT),
        cost_estimate=pl.CostEstimate(
            flops=4 * blocks * slots * BLOCK * BLOCK * HEAD,
            bytes_accessed=14 << 20,
            transcendentals=blocks * slots * BLOCK * BLOCK,
        ),
        name="forward",
    )(links, sink, rows)


def value_grad(links, rows, grads, attended, weights, sink_weight):
    peers, tokens, _ = grads.shape
    per_device = tokens // BLOCK
    blocks = peers * per_device
    slots = weights.shape[1] // BLOCK
    return pl.pallas_call(
        functools.partial(value_kernel, blocks, slots, per_device),
        out_shape=(
            jax.ShapeDtypeStruct((peers, tokens + EXTRA, HEAD), BF16),
            jax.ShapeDtypeStruct(weights.shape, BF16),
        ),
        in_specs=[SMEM_WHOLE] + [IN_PLACE] * 4 + [VMEM_WHOLE],
        out_specs=(IN_PLACE, IN_PLACE),
        scratch_shapes=[
            pltpu.VMEM((blocks, BLOCK), F32),
            pltpu.VMEM((peers, tokens, HEAD), BF16),
            pltpu.VMEM((peers, tokens, HEAD), BF16),
            pltpu.VMEM((peers, tokens, HEAD), BF16),
            pltpu.VMEM(weights.shape, BF16),
            pltpu.VMEM(weights.shape, BF16),
            pltpu.VMEM((blocks, BLOCK, HEAD), F32),
            pltpu.VMEM((peers, tokens + EXTRA, HEAD), BF16),
            pltpu.SemaphoreType.DMA((3, 4)),
            pltpu.SemaphoreType.DMA,
            pltpu.SemaphoreType.DMA((4,)),
            pltpu.SemaphoreType.DMA,
        ],
        compiler_params=pltpu.CompilerParams(vmem_limit_bytes=VMEM_GRANT),
        cost_estimate=pl.CostEstimate(
            flops=4 * blocks * slots * BLOCK * BLOCK * HEAD,
            bytes_accessed=20 << 20,
            transcendentals=0,
        ),
        name="value_grad",
    )(links, rows, grads, attended, weights, sink_weight)


def backward(links, rows, changes, scaling):
    peers, depth, _ = rows.shape
    tokens = depth // 3
    per_device = tokens // BLOCK
    blocks = peers * per_device
    slots = changes.shape[1] // BLOCK
    return pl.pallas_call(
        functools.partial(backward_kernel, blocks, slots, per_device, scaling),
        out_shape=jax.ShapeDtypeStruct((peers, 2 * tokens, HEAD), BF16),
        in_specs=[SMEM_WHOLE, IN_PLACE, IN_PLACE],
        out_specs=IN_PLACE,
        scratch_shapes=[
            pltpu.VMEM((blocks, BLOCK, HEAD), F32),
            pltpu.VMEM((peers, 2 * tokens, HEAD), BF16),
            pltpu.VMEM(changes.shape, BF16),
            pltpu.VMEM((peers, 2 * tokens, HEAD), BF16),
            pltpu.SemaphoreType.DMA((4,)),
            pltpu.SemaphoreType.DMA,
            pltpu.SemaphoreType.DMA((4,)),
        ],
        compiler_params=pltpu.CompilerParams(vmem_limit_bytes=VMEM_GRANT),
        cost_estimate=pl.CostEstimate(
            flops=4 * blocks * slots * BLOCK * BLOCK * HEAD,
            bytes_accessed=12 << 20,
            transcendentals=0,
        ),
        name="backward",
    )(links, rows, changes)


def pack_kernel(*refs):
    *sources, out, flat, split, load_sem, send_sem = refs
    heads, tokens = split.shape[1], split.shape[2]
    loads, sends = [], []
    for part, source in enumerate(sources):
        loads.append(pltpu.make_async_copy(source.at[0], flat.at[part], load_sem.at[part]))
        span = out.at[:, pl.ds(part * tokens, tokens), :]
        sends.append(pltpu.make_async_copy(split.at[part], span, send_sem.at[part]))
        loads[part].start()
    for part in range(len(sources)):
        loads[part].wait()
        for h in range(heads):
            split[part, h] = flat[part, :, pl.ds(h * HEAD, HEAD)]
        sends[part].start()
    for send in sends:
        send.wait()


def pack(*arrays):
    _, tokens, columns = arrays[0].shape
    heads, count = columns // HEAD, len(arrays)
    return pl.pallas_call(
        pack_kernel,
        out_shape=jax.ShapeDtypeStruct((heads, count * tokens, HEAD), arrays[0].dtype),
        in_specs=[IN_PLACE] * count,
        out_specs=IN_PLACE,
        scratch_shapes=[
            pltpu.VMEM((count, tokens, columns), arrays[0].dtype),
            pltpu.VMEM((count, heads, tokens, HEAD), arrays[0].dtype),
            pltpu.SemaphoreType.DMA((count,)),
            pltpu.SemaphoreType.DMA((count,)),
        ],
        compiler_params=pltpu.CompilerParams(vmem_limit_bytes=VMEM_GRANT),
        cost_estimate=pl.CostEstimate(
            flops=0, bytes_accessed=4 * count * tokens * columns, transcendentals=0),
        name="pack",
    )(*arrays)


def unpack_kernel(source, *refs):
    *outs, split, flat, load_sem, send_sem = refs
    heads, tokens = source.shape[0], flat.shape[1]
    loads, sends = [], []
    for part, out in enumerate(outs):
        span = source.at[:, pl.ds(part * tokens, tokens), :]
        loads.append(pltpu.make_async_copy(span, split.at[part], load_sem.at[part]))
        sends.append(pltpu.make_async_copy(flat.at[part], out.at[0], send_sem.at[part]))
        loads[part].start()
    for part in range(len(outs)):
        loads[part].wait()
        for h in range(heads):
            flat[part, :, pl.ds(h * HEAD, HEAD)] = split[part, h]
        sends[part].start()
    for send in sends:
        send.wait()


def unpack(array, tokens, count):
    heads = array.shape[0]
    return pl.pallas_call(
        unpack_kernel,
        out_shape=(jax.ShapeDtypeStruct((1, tokens, heads * HEAD), array.dtype),) * count,
        in_specs=[IN_PLACE],
        out_specs=(IN_PLACE,) * count,
        scratch_shapes=[
            pltpu.VMEM((count, heads, tokens, HEAD), array.dtype),
            pltpu.VMEM((count, tokens, heads * HEAD), array.dtype),
            pltpu.SemaphoreType.DMA((count,)),
            pltpu.SemaphoreType.DMA((count,)),
        ],
        compiler_params=pltpu.CompilerParams(vmem_limit_bytes=56 << 20),
        cost_estimate=pl.CostEstimate(
            flops=0, bytes_accessed=4 * heads * count * tokens * HEAD, transcendentals=0),
        name="unpack",
    )(array)


def unpack_last_kernel(source, *refs):
    *outs, flat, send_sem = refs
    heads, tokens = source.shape[0], flat.shape[1]
    sends = []
    for part, out in enumerate(outs):
        for h in range(heads):
            flat[part, :, pl.ds(h * HEAD, HEAD)] = source[h, pl.ds(part * tokens, tokens), :]
        sends.append(pltpu.make_async_copy(flat.at[part], out.at[0], send_sem.at[part]))
        sends[part].start()
    for send in sends:
        send.wait()


def unpack_last(array, tokens, count):
    heads = array.shape[0]
    return pl.pallas_call(
        unpack_last_kernel,
        out_shape=(jax.ShapeDtypeStruct((1, tokens, heads * HEAD), array.dtype),) * count,
        in_specs=[VMEM_WHOLE],
        out_specs=(IN_PLACE,) * count,
        scratch_shapes=[
            pltpu.VMEM((count, tokens, heads * HEAD), array.dtype),
            pltpu.SemaphoreType.DMA((count,)),
        ],
        compiler_params=pltpu.CompilerParams(vmem_limit_bytes=8 << 20),
        cost_estimate=pl.CostEstimate(
            flops=0, bytes_accessed=4 * heads * count * tokens * HEAD, transcendentals=0),
        name="unpack_last",
    )(array)


def exchange(array):
    return lax.all_to_all(array, "seq", split_axis=0, concat_axis=0, tiled=True)


def sum_over_documents(values):
    size = lax.axis_size("dp")
    stride = 1
    while stride < size:
        width = min(4, size // stride)
        shifted = []
        for k in range(1, width):
            pairs = []
            for i in range(size):
                digit = i // stride % width
                pairs.append((i, i + ((digit + k) % width - digit) * stride))
            shifted.append(lax.ppermute(values, "dp", pairs))
        values = functools.reduce(jnp.add, shifted, values)
        stride *= width
    return values


def on_device(query_rows, key_rows, value_rows, sink_logit, grad_out, pattern):
    heads, blocks, slots = pattern.shape
    head = lax.axis_index("seq")
    links = lax.dynamic_index_in_dim(pattern, head, 0, keepdims=False).reshape(blocks * slots)
    sink = lax.dynamic_slice_in_dim(sink_logit, head, 1, 0)
    scaling = HEAD ** -0.5

    tokens = query_rows.shape[1]
    grad_out, links, sink = lax.optimization_barrier((grad_out, links, sink))
    rows = exchange(pack(query_rows, key_rows, value_rows))
    grads = exchange(pack(grad_out))
    attended, weights, sink_weight = forward(links, sink, rows, scaling, slots)
    attended_tokens = exchange(attended)
    values, changes = value_grad(links, rows, grads, attended, weights, sink_weight)
    attended_tokens, values, changes = lax.optimization_barrier((attended_tokens, values, changes))
    value_tokens = exchange(values)
    others = backward(links, rows, changes, scaling)
    value_tokens, others = lax.optimization_barrier((value_tokens, others))
    other_tokens = exchange(others)

    addends = value_tokens[:, tokens:tokens + 3, 0].astype(F32)
    grad_sink = sum_over_documents(jnp.sum(addends, axis=1)) / lax.axis_size("dp")
    (out,) = unpack(attended_tokens, tokens, 1)
    (grad_value,) = unpack(value_tokens, tokens, 1)
    grad_query, grad_key = unpack_last(other_tokens, tokens, 2)
    return out, grad_query, grad_key, grad_value, grad_sink


def solution(mesh):
    placed = (
        P("dp", "seq", None),
        P("dp", "seq", None),
        P("dp", "seq", None),
        P(),
        P("dp", "seq", None),
        P(),
    )
    return jax.shard_map(
        on_device,
        mesh=mesh,
        in_specs=placed,
        out_specs=(
            P("dp", "seq", None),
            P("dp", "seq", None),
            P("dp", "seq", None),
            P("dp", "seq", None),
            P(),
        ),
        check_vma=False,
    )
```
